32 devices in a mesh: lat: 8 (over z, x), lon: 4 (over y, core).
Axes of the slice: x: 2, y: 2, z: 4, core: 2. Of those that a mesh axis runs over, the one named last changes fastest.
Arguments:
- state: bfloat16 [32, 32, 64, 128], P('lat', 'lon'), may hold values from -6 to 6
- obs_row: int32 [32, 32, 128], P('lat', 'lon'), may hold values from 0 to 63
- obs_count: int32 [32, 32], P('lat', 'lon'), may hold values from 0 to 128
- obs_value: float32 [32, 32, 128], P('lat', 'lon'), may hold values from -6 to 6
- obs_weight: float32 [32, 32, 128], P('lat', 'lon'), may hold values from 0.5 to 2
- quadrant: int32 [32, 32, 64], P('lat', 'lon'), may hold values from 0 to 3
- frac_lat: float32 [32, 32, 64], P('lat', 'lon'), may hold values from 0 to 1
- frac_lon: float32 [32, 32, 64], P('lat', 'lon'), may hold values from 0 to 1
- land: int32 [32, 32, 64], P('lat', 'lon'), may hold values 0 or 1
Outputs:
- analysis: bfloat16 [32, 32, 64, 128], P('lat', 'lon')
The draws below stay inside these ranges and needn't reach their ends.
All inputs are finite; a program needn't handle non-finite values. No bound on the sum of `land` on one device may be relied on, other than what follows from the above.
Results may differ from the reference program's by a relative error of at most 0.0051.
Values may be sent and summed in bfloat16 or wider, within the bound.
A program may use at most 64 MiB of HBM per device.

```python
import math
import jax
import jax.numpy as jnp
from jax import lax

M = 128
OBS = 128
RC = 64
ITERS = 6
NLAT = 32
NLON = 32


def touch_ends(values, own_key, low, largest):
    dims = values.shape
    place = [jax.random.randint(jax.random.fold_in(own_key, axis), (), 0, dims[axis]) for axis in range(len(dims))]
    values = values.at[tuple(place)].set(low)
    longest = dims.index(max(dims))
    place[longest] = (place[longest] + 1) % dims[longest]
    return values.at[tuple(place)].set(largest)


def block_levels(rng, extent, cuts, low, top_value):
    def one(position, shards_of):
        steps = jax.random.uniform(jax.random.fold_in(jax.random.fold_in(rng, 6), position), (shards_of,), jnp.float32, low / len(cuts), top_value / len(cuts))
        return jnp.repeat(jnp.exp(steps), extent[position] // shards_of).reshape((-1,) + (1,) * (len(extent) - position - 1))

    level = one(*cuts[0])
    for cut in cuts[1:]:
        level = level * one(*cut)
    return level


def gaussian(rng, shape, spread, bound, shards=(), kind=jnp.bfloat16):
    level = block_levels(rng, shape, shards, -0.22, 0.18) if shards else 1.0
    values = jax.random.normal(rng, shape, jnp.float32) * spread * level
    return jnp.minimum(jnp.maximum(values, -bound), bound).astype(kind)


def setup_inputs(seed: int = 0) -> dict:
    keys = jax.random.split(jax.random.key(seed), 10)
    return {
        "state": gaussian(keys[0], (NLAT, NLON, RC, M), 1.0, 6.0, ((0, 8), (1, 4))),
        "obs_row": touch_ends(jax.random.randint(keys[1], (NLAT, NLON, OBS), 0, RC), jax.random.fold_in(keys[1], 1), 0, RC - 1).astype(jnp.int32),
        "obs_count": touch_ends(jax.random.randint(keys[2], (NLAT, NLON), 0, OBS + 1), jax.random.fold_in(keys[2], 1), 0, OBS).astype(jnp.int32),
        "obs_value": gaussian(keys[3], (NLAT, NLON, OBS), 1.0, 6.0, ((0, 8), (1, 4)), jnp.float32),
        "obs_weight": jnp.clip(jnp.exp(math.log(2.0) - 1.3862944 * jax.random.uniform(keys[4], (NLAT, NLON, OBS), jnp.float32) ** block_levels(keys[4], (NLAT, NLON, OBS), ((0, 8), (1, 4)), -0.2, 0.2)), 0.5, 2.0),
        "quadrant": touch_ends(jax.random.randint(keys[5], (NLAT, NLON, RC), 0, 4), jax.random.fold_in(keys[5], 1), 0, 3).astype(jnp.int32),
        "frac_lat": jnp.clip(1.0 * jax.random.uniform(keys[6], (NLAT, NLON, RC), jnp.float32) ** block_levels(keys[6], (NLAT, NLON, RC), ((0, 8), (1, 4)), -0.2, 0.2), 0.0, 1.0),
        "frac_lon": jnp.clip(1.0 * jax.random.uniform(keys[7], (NLAT, NLON, RC), jnp.float32) ** block_levels(keys[7], (NLAT, NLON, RC), ((0, 8), (1, 4)), -0.2, 0.2), 0.0, 1.0),
        "land": touch_ends((jax.random.randint(keys[8], (NLAT, NLON, RC), 0, 4) < 3).astype(jnp.int32), jax.random.fold_in(keys[8], 1), 0, 1),
    }


HIGHEST = lax.Precision.HIGHEST
NEAR_WEIGHTS = (0.5, 1.0, 0.5)

def node_terms(cells, member_mean, obs_rows, counts, observed, weight):
    picked = jnp.take_along_axis(cells, obs_rows[..., None], axis=-2).astype(jnp.float32)
    centre = jnp.take_along_axis(member_mean, obs_rows, axis=-1)
    slot_ids = lax.broadcasted_iota(jnp.int32, obs_rows.shape, obs_rows.ndim - 1)
    live_weight = jnp.where(slot_ids < counts[..., None], weight, jnp.float32(0.0))
    blocks = ((picked - centre[..., None]) * live_weight[..., None]).astype(jnp.bfloat16)
    innovation = ((observed - centre) * live_weight).astype(jnp.bfloat16)
    return (blocks, innovation)

def gram_terms(blocks, innovation):
    wide_blocks = blocks.astype(jnp.float32)
    node_grams = jnp.einsum('...sm,...sn->...mn', wide_blocks, wide_blocks)
    node_sides = jnp.einsum('...sm,...s->...m', wide_blocks, innovation.astype(jnp.float32))
    return (node_grams, node_sides)

def transform_weights(gram_sum, side_sum, members):
    identity = jnp.eye(members, dtype=jnp.float32)
    frob_norm = jnp.sqrt(lax.optimization_barrier(jnp.sum(gram_sum * gram_sum, axis=(-2, -1))))
    iterate = gram_sum / frob_norm[..., None, None]
    inv_root = jnp.broadcast_to(identity, gram_sum.shape)
    for newton_step in range(ITERS):
        factor = 1.5 * identity - 0.5 * jnp.einsum('...ab,...bc->...ac', inv_root, iterate, precision=HIGHEST)
        iterate = jnp.einsum('...ab,...bc->...ac', iterate, factor, precision=HIGHEST)
        inv_root = jnp.einsum('...ab,...bc->...ac', factor, inv_root, precision=HIGHEST)
    inner_term = jnp.einsum('...ab,...b->...a', inv_root, side_sum, precision=HIGHEST)
    mean_weight = jnp.einsum('...ab,...b->...a', inv_root, inner_term, precision=HIGHEST) / frob_norm[..., None]
    spread_part = math.sqrt(members - 1) * inv_root / jnp.sqrt(frob_norm)[..., None, None]
    return (mean_weight[..., :, None] + spread_part).astype(jnp.bfloat16)

def reference(state, obs_row, obs_count, obs_value, obs_weight, quadrant, frac_lat, frac_lon, land):
    members = state.shape[3]
    row_ids = jnp.arange(NLAT, dtype=jnp.int32)

    def pick(array, row_index):
        return lax.dynamic_index_in_dim(array, row_index, 0, keepdims=False)

    def terms_row(row_index):
        cells = pick(state, row_index)
        member_mean = lax.optimization_barrier(jnp.mean(cells.astype(jnp.float32), axis=-1))
        return node_terms(cells, member_mean, pick(obs_row, row_index), pick(obs_count, row_index), pick(obs_value, row_index), pick(obs_weight, row_index))
    blocks, innovation = lax.map(terms_row, row_ids)
    padded_blocks = jnp.pad(blocks, ((1, 1), (0, 0), (0, 0), (0, 0)))
    padded_innov = jnp.pad(innovation, ((1, 1), (0, 0), (0, 0)))

    def weight_row(row_index):
        near_blocks = lax.dynamic_slice_in_dim(padded_blocks, row_index, 3, 0)
        near_innov = lax.dynamic_slice_in_dim(padded_innov, row_index, 3, 0)
        node_grams, node_sides = gram_terms(near_blocks, near_innov)
        identity = jnp.eye(members, dtype=jnp.float32)
        gram_sum = jnp.zeros((NLON, members, members), jnp.float32) + (members - 1) * identity
        side_sum = jnp.zeros((NLON, members), jnp.float32)
        for lat_off in range(3):
            for lon_off in range(3):
                factor = NEAR_WEIGHTS[lat_off] * NEAR_WEIGHTS[lon_off]
                gram_sum = gram_sum + factor * jnp.roll(node_grams[lat_off], 1 - lon_off, axis=0)
                side_sum = side_sum + factor * jnp.roll(node_sides[lat_off], 1 - lon_off, axis=0)
        return transform_weights(gram_sum, side_sum, members)
    weights = lax.map(weight_row, row_ids)
    padded_weights = jnp.pad(weights, ((1, 1), (0, 0), (0, 0), (0, 0)))

    def analysis_row(row_index):
        near_weights = lax.dynamic_slice_in_dim(padded_weights, row_index, 3, 0)
        cells = pick(state, row_index)
        values = cells.astype(jnp.float32)
        member_mean = lax.optimization_barrier(jnp.mean(values, axis=-1))
        perturb = (values - member_mean[..., None]).astype(jnp.bfloat16)
        corner_ids = pick(quadrant, row_index)
        lat_half = corner_ids // 2
        lon_half = corner_ids % 2
        lat_frac = pick(frac_lat, row_index)
        lon_frac = pick(frac_lon, row_index)
        accumulated = jnp.zeros(values.shape, jnp.float32)
        for lat_off in range(3):
            along_lat = jnp.where(lat_half == lat_off, 1.0 - lat_frac, 0.0) + jnp.where(lat_half + 1 == lat_off, lat_frac, 0.0)
            for lon_off in range(3):
                along_lon = jnp.where(lon_half == lon_off, 1.0 - lon_frac, 0.0) + jnp.where(lon_half + 1 == lon_off, lon_frac, 0.0)
                shifted = jnp.roll(near_weights[lat_off], 1 - lon_off, axis=0)
                product = jnp.einsum('jrm,jmn->jrn', perturb.astype(jnp.float32), shifted.astype(jnp.float32))
                accumulated = accumulated + (along_lat * along_lon)[..., None] * product
        land_row = pick(land, row_index)
        result = jnp.where(land_row[..., None] == 1, member_mean[..., None] + accumulated, values)
        return result.astype(jnp.bfloat16)
    return lax.map(analysis_row, row_ids)
```

```python
import functools
import math

import jax
import jax.numpy as jnp
from jax import lax
from jax.experimental import pallas as pl
from jax.experimental.pallas import tpu as pltpu
from jax.sharding import PartitionSpec as P

ITERS = 6
NEAR = (0.5, 1.0, 0.5)
SIDE_ROWS = 16
F32 = jnp.float32
BF16 = jnp.bfloat16
MESH = pl.DeviceIdType.MESH
WAYS = ((-1, 0), (1, 0), (-1, -1), (-1, 1), (1, -1), (1, 1), (0, -1), (0, 1))


def nn(a, b):
    return lax.dot_general(a, b, (((1,), (0,)), ((), ())), preferred_element_type=F32)


def nt(a, b):
    return lax.dot_general(a, b, (((1,), (1,)), ((), ())), preferred_element_type=F32)


def tn(a, b):
    return lax.dot_general(a, b, (((0,), (0,)), ((), ())), preferred_element_type=F32)


def group_of(count, most=4):
    return next(g for g in range(most, 0, -1) if count % g == 0)


def prep_kernel(count_ref, state_ref, row_ref, value_ref, weight_ref, out_ref):
    tile_lat, tile_lon, cells, members = state_ref.shape
    slots = row_ref.shape[-1]
    nodes = tile_lat * tile_lon
    group = group_of(nodes)

    def step(t, carry):
        for g in range(group):
            node = t * group + g
            i, j = node // tile_lon, node % tile_lon
            values = state_ref[i, j].astype(F32)
            mean = jnp.sum(values, axis=1, keepdims=True) * (1.0 / members)
            pert = values - mean
            lane = lax.broadcasted_iota(jnp.int32, (1, slots), 1)
            weight = jnp.where(lane < count_ref[i, j], weight_ref[i, pl.ds(j, 1), :], 0.0)
            square = weight * weight
            hit = row_ref[i, pl.ds(j, 1), :] == lax.broadcasted_iota(jnp.int32, (cells, slots), 0)
            density = jnp.sum(jnp.where(hit, square, 0.0), axis=1, keepdims=True)
            pulled = jnp.sum(
                jnp.where(hit, square * value_ref[i, pl.ds(j, 1), :], 0.0), axis=1, keepdims=True
            )
            out_ref[i, j, pl.ds(0, cells), :] = (jnp.sqrt(density) * pert).astype(BF16)
            side = jnp.sum(pert * (pulled - density * mean), axis=0, keepdims=True)
            high = side.astype(BF16).astype(F32)
            which = lax.broadcasted_iota(jnp.int32, (SIDE_ROWS, members), 0)
            tail = jnp.where(which == 0, high, jnp.where(which == 1, side - high, 0.0))
            out_ref[i, j, pl.ds(cells, SIDE_ROWS), :] = tail.astype(BF16)
        return carry

    lax.fori_loop(0, nodes // group, step, 0)


def edge_slices(step, size):
    if step == 0:
        return slice(0, size), slice(1, size + 1), size
    if step < 0:
        return 0, size + 1, 1
    return size - 1, 0, 1


def main_kernel(
    counts, qx_ref, state_ref, quadrant_ref, frac_lat_ref, frac_lon_ref, land_ref,
    out_ref, qbuf, wbuf, q_send, q_recv, w_send, w_recv,
):
    n_lat, n_lon = counts
    tile_lat, tile_lon, cells, members = state_ref.shape
    lat, lon = lax.axis_index("lat"), lax.axis_index("lon")

    def exists(way):
        if way[0] < 0:
            return lat > 0
        if way[0] > 0:
            return lat < n_lat - 1
        return None

    def where_exists(way, do):
        if way[0] == 0:
            do()
        else:
            pl.when(exists(way))(do)

    def peer(way):
        return (lat + way[0], lax.rem(lon + way[1] + n_lon, n_lon))

    def at(ref, i, j):
        i = pl.ds(i.start, i.stop - i.start) if isinstance(i, slice) else i
        j = pl.ds(j.start, j.stop - j.start) if isinstance(j, slice) else j
        return ref.at[i, j]

    def copy(source, offset, buffer, send, recv, index):
        way = WAYS[index]
        si, di, _ = edge_slices(way[0], tile_lat)
        sj, dj, _ = edge_slices(way[1], tile_lon)

        def moved(s):
            return slice(s.start + offset, s.stop + offset) if isinstance(s, slice) else s + offset

        return pltpu.make_async_remote_copy(
            src_ref=at(source, moved(si), moved(sj)),
            dst_ref=at(buffer, di, dj),
            send_sem=send.at[index],
            recv_sem=recv.at[index],
            device_id=peer(way),
            device_id_type=MESH,
        )

    def q_copy(index):
        return copy(qx_ref, 0, qbuf, q_send, q_recv, index)

    def w_copy(index):
        return copy(wbuf, 1, wbuf, w_send, w_recv, index)

    barrier = pltpu.get_barrier_semaphore()
    for way in WAYS:
        where_exists(way, lambda way=way: pl.semaphore_signal(
            barrier, inc=1, device_id=peer(way), device_id_type=MESH))
    present = 2 + 3 * (lat > 0).astype(jnp.int32) + 3 * (lat < n_lat - 1).astype(jnp.int32)
    pl.semaphore_wait(barrier, present)
    for index, way in enumerate(WAYS):
        where_exists(way, lambda index=index: q_copy(index).start())

    @pl.when(lat == 0)
    def _():
        qbuf[0] = jnp.zeros(qbuf.shape[1:], BF16)
        wbuf[0] = jnp.zeros(wbuf.shape[1:], BF16)

    @pl.when(lat == n_lat - 1)
    def _():
        qbuf[tile_lat + 1] = jnp.zeros(qbuf.shape[1:], BF16)
        wbuf[tile_lat + 1] = jnp.zeros(wbuf.shape[1:], BF16)

    for i in range(tile_lat):
        qbuf[i + 1, pl.ds(1, tile_lon)] = qx_ref[i]

    def received(index, make):
        way = WAYS[index]
        back = (-way[0], -way[1])
        where_exists(back, lambda: make(index).wait_recv())

    def sent(index, make):
        where_exists(WAYS[index], lambda: make(index).wait_send())

    eye = (
        lax.broadcasted_iota(jnp.int32, (members, members), 0)
        == lax.broadcasted_iota(jnp.int32, (members, members), 1)
    ).astype(F32)

    def gram_of(i, j):
        left, right = [], []
        tail = jnp.zeros((SIDE_ROWS, members), F32)
        for b in range(3):
            for a in range(3):
                scale = NEAR[a] * NEAR[b]
                block = qbuf[i + a, j + b, pl.ds(0, cells), :]
                right.append(block)
                left.append(block if scale == 1.0 else block * jnp.asarray(scale, BF16))
                tail += scale * qbuf[i + a, j + b, pl.ds(cells, SIDE_ROWS), :].astype(F32)
        gram = tn(jnp.concatenate(left, axis=0), jnp.concatenate(right, axis=0))
        side = jnp.sum(tail, axis=0, keepdims=True)
        return gram + (members - 1.0) * eye, side

    def total(x):
        return jnp.sum(jnp.sum(x, axis=0, keepdims=True), axis=1, keepdims=True)

    def transform(places):
        grams, sides, frobs, spots = [], [], [], []
        for i, j in places:
            gram, side = gram_of(i, j)
            grams.append(gram)
            sides.append(side)
        cy, ey, cz, ez = [], [], [], []
        for gram in grams:
            frob = jnp.sqrt(total(gram * gram))
            frobs.append(frob)
            scaled = gram * (1.0 / frob)
            centre = total(scaled * eye) * (1.0 / members)
            rest = scaled - centre * eye
            cf, ef = 1.5 - 0.5 * centre, -0.5 * rest
            prod = nn(ef.astype(BF16), rest.astype(BF16))
            cy.append(cf * centre)
            ey.append(prod + cf * rest + centre * ef)
            cz.append(cf)
            ez.append(ef)
        for step in range(1, ITERS):
            last = step == ITERS - 1
            ybs = [e.astype(BF16) for e in ey]
            zbs = [e.astype(BF16) for e in ez]
            prods = [nn(zb, yb) for zb, yb in zip(zbs, ybs)]
            cfs = [1.5 - 0.5 * (y * z) for y, z in zip(cy, cz)]
            efs = [
                -0.5 * (prods[n] + cz[n] * ey[n] + cy[n] * ez[n]) for n in range(len(places))
            ]
            fbs = [e.astype(BF16) for e in efs]
            if last:
                both = [nn(fb, zb) for fb, zb in zip(fbs, zbs)]
            else:
                both = [
                    nn(fb, jnp.concatenate([zb, yb], axis=1))
                    for fb, zb, yb in zip(fbs, zbs, ybs)
                ]
            for n in range(len(places)):
                if not last:
                    ey[n] = both[n][:, members:] + cfs[n] * ey[n] + cy[n] * efs[n]
                    cy[n] = cfs[n] * cy[n]
                ez[n] = both[n][:, :members] + cfs[n] * ez[n] + cz[n] * efs[n]
                cz[n] = cfs[n] * cz[n]
        for n, (i, j) in enumerate(places):
            root = ez[n] + cz[n] * eye
            high = root.astype(BF16)
            low = (root - high.astype(F32)).astype(BF16)
            pair = jnp.concatenate([high, low], axis=1)
            side = jnp.broadcast_to(sides[n], (members, members))
            s_high = side.astype(BF16)
            s_low = (side - s_high.astype(F32)).astype(BF16)
            inner = nt(pair, jnp.concatenate([s_high, s_high], axis=1)) + nt(high, s_low)
            i_high = inner.astype(BF16)
            i_low = (inner - i_high.astype(F32)).astype(BF16)
            mean_weight = nn(pair, jnp.concatenate([i_high, i_high], axis=0)) + nn(high, i_low)
            inv = 1.0 / frobs[n]
            weights = mean_weight * inv + (math.sqrt(members - 1) * jnp.sqrt(inv)) * root
            wbuf[i + 1, j + 1] = weights.astype(BF16)

    mid_lat, mid_lon = tile_lat - 2, tile_lon - 2
    n_rows, n_sides, n_inner = 2 * tile_lon, 2 * mid_lat, mid_lat * mid_lon
    group = next(g for g in (4, 2) if n_rows % g == 0 and n_sides % g == 0 and n_inner % g == 0)
    ahead = n_inner // group // 3
    g_rows, g_sides, g_inner = n_rows // group, n_sides // group, n_inner // group

    def row_place(k):
        return (k % 2) * (tile_lat - 1), k // 2

    def side_place(k):
        return 1 + k // 2, (k % 2) * (tile_lon - 1)

    def inner_place(k):
        return 1 + k // mid_lon, 1 + k % mid_lon

    def place(slot, g):
        rows = slot - ahead
        sides = rows - g_rows
        after = slot - g_rows - g_sides
        is_inner = (slot < ahead) | (sides >= g_sides)
        inner = inner_place(jnp.where(slot < ahead, slot, jnp.maximum(after, 0)) * group + g)
        row = row_place(jnp.clip(rows, 0, g_rows - 1) * group + g)
        side = side_place(jnp.clip(sides, 0, g_sides - 1) * group + g)
        i = jnp.where(is_inner, inner[0], jnp.where(sides >= 0, side[0], row[0]))
        j = jnp.where(is_inner, inner[1], jnp.where(sides >= 0, side[1], row[1]))
        return i, j

    def node_step(slot, carry):
        @pl.when(slot == ahead)
        def _():
            for index in range(len(WAYS)):
                received(index, q_copy)

        transform([place(slot, g) for g in range(group)])

        @pl.when(slot == ahead + g_rows - 1)
        def _():
            for index in range(6):
                where_exists(WAYS[index], lambda index=index: w_copy(index).start())

        @pl.when(slot == ahead + g_rows + g_sides - 1)
        def _():
            for index in range(6, 8):
                w_copy(index).start()

        return carry

    lax.fori_loop(0, g_rows + g_sides + g_inner, node_step, 0)

    def analyse(i, j):
        values = state_ref[i, j].astype(F32)
        mean = jnp.sum(values, axis=1, keepdims=True) * (1.0 / members)
        pert = (values - mean).astype(BF16)
        corner = quadrant_ref[i, pl.ds(j, 1), :]
        along = []
        for half, frac in (
            (corner // 2, frac_lat_ref[i, pl.ds(j, 1), :]),
            (corner % 2, frac_lon_ref[i, pl.ds(j, 1), :]),
        ):
            for a in range(3):
                along.append(
                    jnp.where(half == a, 1.0 - frac, 0.0) + jnp.where(half + 1 == a, frac, 0.0)
                )
        along.append(land_ref[i, pl.ds(j, 1), :].astype(F32))
        along.append(jnp.zeros_like(along[0]))
        coef = jnp.transpose(jnp.concatenate(along, axis=0))
        acc = mean
        for a in range(3):
            wide = jnp.concatenate([wbuf[i + a, j + b] for b in range(3)], axis=1)
            prod = nn(pert, wide)
            row = sum(
                coef[:, 3 + b : 4 + b] * prod[:, b * members : (b + 1) * members] for b in range(3)
            )
            acc = acc + coef[:, a : a + 1] * row
        result = jnp.where(coef[:, 6:7] == 1.0, acc, values)
        out_ref[i, j] = result.astype(BF16)

    def inner_step(t, carry):
        for g in range(group):
            analyse(*inner_place(t * group + g))
        return carry

    lax.fori_loop(0, g_inner, inner_step, 0)
    for index in range(len(WAYS)):
        received(index, w_copy)

    def rim_step(t, carry):
        for g in range(group):
            k = t * group + g
            row, side = row_place(jnp.minimum(k, n_rows - 1)), side_place(jnp.maximum(k - n_rows, 0))
            analyse(jnp.where(k < n_rows, row[0], side[0]), jnp.where(k < n_rows, row[1], side[1]))
        return carry

    lax.fori_loop(0, g_rows + g_sides, rim_step, 0)
    for index in range(len(WAYS)):
        sent(index, q_copy)
        sent(index, w_copy)


VM = pl.BlockSpec(memory_space=pltpu.VMEM)


def body(counts, state, obs_row, obs_count, obs_value, obs_weight, quadrant, frac_lat, frac_lon, land):
    tile_lat, tile_lon, cells, members = state.shape
    rows = cells + SIDE_ROWS
    qx = pl.pallas_call(
        prep_kernel,
        out_shape=jax.ShapeDtypeStruct((tile_lat, tile_lon, rows, members), BF16),
        in_specs=[pl.BlockSpec(memory_space=pltpu.SMEM)] + [VM] * 4,
        out_specs=VM,
        name="prep",
    )(obs_count, state, obs_row, obs_value, obs_weight)
    return pl.pallas_call(
        functools.partial(main_kernel, counts),
        out_shape=jax.ShapeDtypeStruct(state.shape, BF16),
        in_specs=[VM] * 6,
        out_specs=VM,
        scratch_shapes=[
            pltpu.VMEM((tile_lat + 2, tile_lon + 2, rows, members), BF16),
            pltpu.VMEM((tile_lat + 2, tile_lon + 2, members, members), BF16),
            pltpu.SemaphoreType.DMA((8,)),
            pltpu.SemaphoreType.DMA((8,)),
            pltpu.SemaphoreType.DMA((8,)),
            pltpu.SemaphoreType.DMA((8,)),
        ],
        compiler_params=pltpu.CompilerParams(
            collective_id=0, has_side_effects=True, vmem_limit_bytes=48 * 1024 * 1024
        ),
        name="analyse",
    )(qx, state, quadrant, frac_lat, frac_lon, land)


def solution(mesh):
    counts = (mesh.shape["lat"], mesh.shape["lon"])
    return jax.shard_map(
        functools.partial(body, counts),
        mesh=mesh,
        in_specs=(
            P("lat", "lon", None, None),
            P("lat", "lon", None),
            P("lat", "lon"),
            P("lat", "lon", None),
            P("lat", "lon", None),
            P("lat", "lon", None),
            P("lat", "lon", None),
            P("lat", "lon", None),
            P("lat", "lon", None),
        ),
        out_specs=P("lat", "lon", None, None),
        check_vma=False,
    )
```

```python
import functools
import math

import jax
import jax.numpy as jnp
from jax import lax
from jax.experimental import pallas as pl
from jax.experimental.pallas import tpu as pltpu
from jax.sharding import PartitionSpec as P

ITERS = 6
NEAR = (0.5, 1.0, 0.5)
SIDE_ROWS = 16
F32 = jnp.float32
BF16 = jnp.bfloat16
MESH = pl.DeviceIdType.MESH
WAYS = ((-1, 0), (1, 0), (-1, -1), (-1, 1), (1, -1), (1, 1), (0, -1), (0, 1))


def nn(a, b):
    return lax.dot_general(a, b, (((1,), (0,)), ((), ())), preferred_element_type=F32)


def nt(a, b):
    return lax.dot_general(a, b, (((1,), (1,)), ((), ())), preferred_element_type=F32)


def tn(a, b):
    return lax.dot_general(a, b, (((0,), (0,)), ((), ())), preferred_element_type=F32)


def group_of(count, most=4):
    return next(g for g in range(most, 0, -1) if count % g == 0)


def prep_kernel(count_ref, state_ref, row_ref, value_ref, weight_ref, out_ref):
    tile_lat, tile_lon, cells, members = state_ref.shape
    slots = row_ref.shape[-1]
    nodes = tile_lat * tile_lon
    group = group_of(nodes)

    def step(t, carry):
        for g in range(group):
            node = t * group + g
            i, j = node // tile_lon, node % tile_lon
            values = state_ref[i, j].astype(F32)
            mean = jnp.sum(values, axis=1, keepdims=True) * (1.0 / members)
            pert = values - mean
            lane = lax.broadcasted_iota(jnp.int32, (1, slots), 1)
            weight = jnp.where(lane < count_ref[i, j], weight_ref[i, pl.ds(j, 1), :], 0.0)
            square = weight * weight
            hit = row_ref[i, pl.ds(j, 1), :] == lax.broadcasted_iota(jnp.int32, (cells, slots), 0)
            density = jnp.sum(jnp.where(hit, square, 0.0), axis=1, keepdims=True)
            pulled = jnp.sum(
                jnp.where(hit, square * value_ref[i, pl.ds(j, 1), :], 0.0), axis=1, keepdims=True
            )
            out_ref[i, j, pl.ds(0, cells), :] = (jnp.sqrt(density) * pert).astype(BF16)
            side = jnp.sum(pert * (pulled - density * mean), axis=0, keepdims=True)
            high = side.astype(BF16).astype(F32)
            which = lax.broadcasted_iota(jnp.int32, (SIDE_ROWS, members), 0)
            tail = jnp.where(which == 0, high, jnp.where(which == 1, side - high, 0.0))
            out_ref[i, j, pl.ds(cells, SIDE_ROWS), :] = tail.astype(BF16)
        return carry

    lax.fori_loop(0, nodes // group, step, 0)


def edge_slices(step, size):
    if step == 0:
        return slice(0, size), slice(1, size + 1), size
    if step < 0:
        return 0, size + 1, 1
    return size - 1, 0, 1


def main_kernel(
    counts, qx_ref, state_ref, quadrant_ref, frac_lat_ref, frac_lon_ref, land_ref,
    out_ref, qbuf, wbuf, q_send, q_recv, w_send, w_recv, r_send, r_recv,
):
    n_lat, n_lon = counts
    row_parts = r_send.shape[1]
    tile_lat, tile_lon, cells, members = state_ref.shape
    lat, lon = lax.axis_index("lat"), lax.axis_index("lon")

    def exists(way):
        if way[0] < 0:
            return lat > 0
        if way[0] > 0:
            return lat < n_lat - 1
        return None

    def where_exists(way, do):
        if way[0] == 0:
            do()
        else:
            pl.when(exists(way))(do)

    def peer(way):
        return (lat + way[0], lax.rem(lon + way[1] + n_lon, n_lon))

    def at(ref, i, j):
        i = pl.ds(i.start, i.stop - i.start) if isinstance(i, slice) else i
        j = pl.ds(j.start, j.stop - j.start) if isinstance(j, slice) else j
        return ref.at[i, j]

    def copy(source, offset, buffer, send, recv, index):
        way = WAYS[index]
        si, di, _ = edge_slices(way[0], tile_lat)
        sj, dj, _ = edge_slices(way[1], tile_lon)

        def moved(s):
            return slice(s.start + offset, s.stop + offset) if isinstance(s, slice) else s + offset

        return pltpu.make_async_remote_copy(
            src_ref=at(source, moved(si), moved(sj)),
            dst_ref=at(buffer, di, dj),
            send_sem=send.at[index],
            recv_sem=recv.at[index],
            device_id=peer(way),
            device_id_type=MESH,
        )

    def q_copy(index):
        return copy(qx_ref, 0, qbuf, q_send, q_recv, index)

    def w_copy(index):
        return copy(wbuf, 1, wbuf, w_send, w_recv, index)

    def row_copy(index, part):
        source, target, _ = edge_slices(WAYS[index][0], tile_lat)
        width = tile_lon // row_parts
        columns = pl.ds(1 + part * width, width)
        return pltpu.make_async_remote_copy(
            src_ref=wbuf.at[source + 1, columns],
            dst_ref=wbuf.at[target, columns],
            send_sem=r_send.at[index, part],
            recv_sem=r_recv.at[index, part],
            device_id=peer(WAYS[index]),
            device_id_type=MESH,
        )

    barrier = pltpu.get_barrier_semaphore()
    for way in WAYS:
        where_exists(way, lambda way=way: pl.semaphore_signal(
            barrier, inc=1, device_id=peer(way), device_id_type=MESH))
    present = 2 + 3 * (lat > 0).astype(jnp.int32) + 3 * (lat < n_lat - 1).astype(jnp.int32)
    pl.semaphore_wait(barrier, present)
    for index, way in enumerate(WAYS):
        where_exists(way, lambda index=index: q_copy(index).start())

    @pl.when(lat == 0)
    def _():
        qbuf[0] = jnp.zeros(qbuf.shape[1:], BF16)
        wbuf[0] = jnp.zeros(wbuf.shape[1:], BF16)

    @pl.when(lat == n_lat - 1)
    def _():
        qbuf[tile_lat + 1] = jnp.zeros(qbuf.shape[1:], BF16)
        wbuf[tile_lat + 1] = jnp.zeros(wbuf.shape[1:], BF16)

    for i in range(tile_lat):
        qbuf[i + 1, pl.ds(1, tile_lon)] = qx_ref[i]

    def received(index, make):
        way = WAYS[index]
        back = (-way[0], -way[1])
        where_exists(back, lambda: make(index).wait_recv())

    def sent(index, make):
        where_exists(WAYS[index], lambda: make(index).wait_send())

    eye = (
        lax.broadcasted_iota(jnp.int32, (members, members), 0)
        == lax.broadcasted_iota(jnp.int32, (members, members), 1)
    ).astype(F32)
    eye_b = eye.astype(BF16)

    def gram_of(i, j):
        left, right = [], []
        tail = jnp.zeros((SIDE_ROWS, members), F32)
        for b in range(3):
            for a in range(3):
                scale = NEAR[a] * NEAR[b]
                block = qbuf[i + a, j + b, pl.ds(0, cells), :]
                right.append(block)
                left.append(block if scale == 1.0 else block * jnp.asarray(scale, BF16))
                tail += scale * qbuf[i + a, j + b, pl.ds(cells, SIDE_ROWS), :].astype(F32)
        gram = tn(jnp.concatenate(left, axis=0), jnp.concatenate(right, axis=0))
        return gram, jnp.sum(tail, axis=0, keepdims=True)

    def total(x):
        return jnp.sum(jnp.sum(x, axis=0, keepdims=True), axis=1, keepdims=True)

    def transform(places):
        group = range(len(places))
        terms = [gram_of(i, j) for i, j in places]
        frobs, cy, ey, cz, ez = [], [], [], [], []
        for gram, _ in terms:
            ridge = members - 1.0
            trace = total(gram * eye)
            frob = jnp.sqrt(total(gram * gram) + 2.0 * ridge * trace + ridge * ridge * members)
            centre = ridge + trace * (1.0 / members)
            inv = 1.0 / centre
            rest = gram * inv + eye * (ridge * inv - 1.0)
            frobs.append(frob)
            start = centre / frob
            cf = 1.5 - 0.5 * start
            ef = rest * (-0.5 * start / cf)
            cy.append(cf * start)
            ey.append((ef + rest) + nn(ef.astype(BF16), rest.astype(BF16)))
            cz.append(cf)
            ez.append(ef)
        for step in range(1, ITERS):
            last = step == ITERS - 1
            ybs = [e.astype(BF16) for e in ey]
            zbs = [e.astype(BF16) for e in ez]
            prods = [nn(zb, yb) for zb, yb in zip(zbs, ybs)]
            cts = [y * z for y, z in zip(cy, cz)]
            cfs = [1.5 - 0.5 * ct for ct in cts]
            efs = [
                ((ey[n] + ez[n]) + prods[n]) * (-0.5 * cts[n] / cfs[n]) for n in group
            ]
            fbs = [e.astype(BF16) for e in efs]
            if last:
                both = [nn(fb, zb) for fb, zb in zip(fbs, zbs)]
            else:
                both = [
                    nn(fb, jnp.concatenate([zb, yb], axis=1))
                    for fb, zb, yb in zip(fbs, zbs, ybs)
                ]
            for n in group:
                if not last:
                    ey[n] = (efs[n] + ey[n]) + both[n][:, members:]
                    cy[n] = cfs[n] * cy[n]
                ez[n] = (efs[n] + ez[n]) + both[n][:, :members]
                cz[n] = cfs[n] * cz[n]
        which = lax.broadcasted_iota(jnp.int32, (SIDE_ROWS, members), 0)
        for n, (i, j) in enumerate(places):
            side = terms[n][1]
            zb = ez[n].astype(BF16)
            high = side.astype(BF16).astype(F32)
            rows = jnp.where(which == 0, high, jnp.where(which == 1, side - high, 0.0))
            inner = side + jnp.sum(nn(rows.astype(BF16), zb), axis=0, keepdims=True)
            inner = inner * (cz[n] * cz[n] / frobs[n])
            high = inner.astype(BF16)
            low = (inner - high.astype(F32)).astype(BF16)
            high = jnp.broadcast_to(high, (members, members))
            low = jnp.broadcast_to(low, (members, members))
            mean_weight = nt(
                jnp.concatenate([zb, eye_b, eye_b], axis=1),
                jnp.concatenate([high, high, low], axis=1),
            )
            spread = math.sqrt(members - 1) * cz[n] / jnp.sqrt(frobs[n])
            wbuf[i + 1, j + 1] = (mean_weight + spread * (ez[n] + eye)).astype(BF16)

    mid_lat, mid_lon = tile_lat - 2, tile_lon - 2
    n_rows, n_sides, n_inner = 2 * tile_lon, 2 * mid_lat, mid_lat * mid_lon
    group = n_rows // row_parts
    ahead = n_inner // group // 3
    g_rows, g_sides, g_inner = n_rows // group, n_sides // group, n_inner // group

    def row_place(k):
        return (k % 2) * (tile_lat - 1), k // 2

    def side_place(k):
        return 1 + k // 2, (k % 2) * (tile_lon - 1)

    def inner_place(k):
        return 1 + k // mid_lon, 1 + k % mid_lon

    def place(slot, g):
        rows = slot - ahead
        sides = rows - g_rows
        after = slot - g_rows - g_sides
        is_inner = (slot < ahead) | (sides >= g_sides)
        inner = inner_place(jnp.where(slot < ahead, slot, jnp.maximum(after, 0)) * group + g)
        row = row_place(jnp.clip(rows, 0, g_rows - 1) * group + g)
        side = side_place(jnp.clip(sides, 0, g_sides - 1) * group + g)
        i = jnp.where(is_inner, inner[0], jnp.where(sides >= 0, side[0], row[0]))
        j = jnp.where(is_inner, inner[1], jnp.where(sides >= 0, side[1], row[1]))
        return i, j

    def node_step(slot, carry):
        @pl.when(slot == ahead)
        def _():
            for index in range(len(WAYS)):
                received(index, q_copy)

        transform([place(slot, g) for g in range(group)])

        for index in range(2):
            part = slot - ahead
            pl.when(exists(WAYS[index]) & (part >= 0) & (part < g_rows))(
                lambda index=index, part=part: row_copy(index, part).start())

        @pl.when(slot == ahead + g_rows - 1)
        def _():
            for index in range(2, 6):
                where_exists(WAYS[index], lambda index=index: w_copy(index).start())

        @pl.when(slot == ahead + g_rows + g_sides - 1)
        def _():
            for index in range(6, 8):
                w_copy(index).start()

        return carry

    lax.fori_loop(0, g_rows + g_sides + g_inner, node_step, 0)

    def analyse(i, j):
        values = state_ref[i, j].astype(F32)
        mean = jnp.sum(values, axis=1, keepdims=True) * (1.0 / members)
        pert = (values - mean).astype(BF16)
        corner = quadrant_ref[i, pl.ds(j, 1), :]
        along = []
        for half, frac in (
            (corner // 2, frac_lat_ref[i, pl.ds(j, 1), :]),
            (corner % 2, frac_lon_ref[i, pl.ds(j, 1), :]),
        ):
            for a in range(3):
                along.append(
                    jnp.where(half == a, 1.0 - frac, 0.0) + jnp.where(half + 1 == a, frac, 0.0)
                )
        along.append(land_ref[i, pl.ds(j, 1), :].astype(F32))
        along.append(jnp.zeros_like(along[0]))
        coef = jnp.transpose(jnp.concatenate(along, axis=0))
        acc = mean
        for a in range(3):
            wide = jnp.concatenate([wbuf[i + a, j + b] for b in range(3)], axis=1)
            prod = nn(pert, wide)
            row = sum(
                coef[:, 3 + b : 4 + b] * prod[:, b * members : (b + 1) * members] for b in range(3)
            )
            acc = acc + coef[:, a : a + 1] * row
        result = jnp.where(coef[:, 6:7] == 1.0, acc, values)
        out_ref[i, j] = result.astype(BF16)

    def inner_step(t, carry):
        for g in range(group):
            analyse(*inner_place(t * group + g))
        return carry

    lax.fori_loop(0, g_inner, inner_step, 0)
    for index in range(2):
        for part in range(row_parts):
            received(index, lambda index, part=part: row_copy(index, part))
    for index in range(2, len(WAYS)):
        received(index, w_copy)

    def rim_step(t, carry):
        for g in range(group):
            k = t * group + g
            row, side = row_place(jnp.minimum(k, n_rows - 1)), side_place(jnp.maximum(k - n_rows, 0))
            analyse(jnp.where(k < n_rows, row[0], side[0]), jnp.where(k < n_rows, row[1], side[1]))
        return carry

    lax.fori_loop(0, g_rows + g_sides, rim_step, 0)
    for index in range(len(WAYS)):
        sent(index, q_copy)
        if index >= 2:
            sent(index, w_copy)
        else:
            for part in range(row_parts):
                sent(index, lambda index, part=part: row_copy(index, part))


VM = pl.BlockSpec(memory_space=pltpu.VMEM)


def body(counts, state, obs_row, obs_count, obs_value, obs_weight, quadrant, frac_lat, frac_lon, land):
    tile_lat, tile_lon, cells, members = state.shape
    rows = cells + SIDE_ROWS
    sizes = (2 * tile_lon, 2 * (tile_lat - 2), (tile_lat - 2) * (tile_lon - 2))
    row_parts = 2 * tile_lon // next(g for g in (4, 2) if all(n % g == 0 for n in sizes))
    qx = pl.pallas_call(
        prep_kernel,
        out_shape=jax.ShapeDtypeStruct((tile_lat, tile_lon, rows, members), BF16),
        in_specs=[pl.BlockSpec(memory_space=pltpu.SMEM)] + [VM] * 4,
        out_specs=VM,
        name="prep",
    )(obs_count, state, obs_row, obs_value, obs_weight)
    return pl.pallas_call(
        functools.partial(main_kernel, counts),
        out_shape=jax.ShapeDtypeStruct(state.shape, BF16),
        in_specs=[VM] * 6,
        out_specs=VM,
        scratch_shapes=[
            pltpu.VMEM((tile_lat + 2, tile_lon + 2, rows, members), BF16),
            pltpu.VMEM((tile_lat + 2, tile_lon + 2, members, members), BF16),
            pltpu.SemaphoreType.DMA((8,)),
            pltpu.SemaphoreType.DMA((8,)),
            pltpu.SemaphoreType.DMA((8,)),
            pltpu.SemaphoreType.DMA((8,)),
            pltpu.SemaphoreType.DMA((2, row_parts)),
            pltpu.SemaphoreType.DMA((2, row_parts)),
        ],
        compiler_params=pltpu.CompilerParams(
            collective_id=0, has_side_effects=True, vmem_limit_bytes=48 * 1024 * 1024
        ),
        name="analyse",
    )(qx, state, quadrant, frac_lat, frac_lon, land)


def solution(mesh):
    counts = (mesh.shape["lat"], mesh.shape["lon"])
    return jax.shard_map(
        functools.partial(body, counts),
        mesh=mesh,
        in_specs=(
            P("lat", "lon", None, None),
            P("lat", "lon", None),
            P("lat", "lon"),
            P("lat", "lon", None),
            P("lat", "lon", None),
            P("lat", "lon", None),
            P("lat", "lon", None),
            P("lat", "lon", None),
            P("lat", "lon", None),
        ),
        out_specs=P("lat", "lon", None, None),
        check_vma=False,
    )
```

```python
import functools
import math

import jax
import jax.numpy as jnp
from jax import lax
from jax.experimental import pallas as pl
from jax.experimental.pallas import tpu as pltpu
from jax.sharding import PartitionSpec as P

ITERS = 6
NEAR = (0.5, 1.0, 0.5)
SIDE_ROWS = 16
F32 = jnp.float32
BF16 = jnp.bfloat16
MESH = pl.DeviceIdType.MESH
WAYS = ((-1, 0), (1, 0), (0, -1), (0, 1))
CORNERS = ((-1, -1), (-1, 1), (1, -1), (1, 1))


def nn(a, b):
    return lax.dot_general(a, b, (((1,), (0,)), ((), ())), preferred_element_type=F32)


def nt(a, b):
    return lax.dot_general(a, b, (((1,), (1,)), ((), ())), preferred_element_type=F32)


def tn(a, b):
    return lax.dot_general(a, b, (((0,), (0,)), ((), ())), preferred_element_type=F32)


def group_of(count, most=4):
    return next(g for g in range(most, 0, -1) if count % g == 0)


def prep_kernel(count_ref, state_ref, row_ref, value_ref, weight_ref, out_ref):
    tile_lat, tile_lon, cells, members = state_ref.shape
    slots = row_ref.shape[-1]
    nodes = tile_lat * tile_lon
    group = group_of(nodes)

    def step(t, carry):
        for g in range(group):
            node = t * group + g
            i, j = node // tile_lon, node % tile_lon
            values = state_ref[i, j].astype(F32)
            mean = jnp.sum(values, axis=1, keepdims=True) * (1.0 / members)
            pert = values - mean
            lane = lax.broadcasted_iota(jnp.int32, (1, slots), 1)
            weight = jnp.where(lane < count_ref[i, j], weight_ref[i, pl.ds(j, 1), :], 0.0)
            square = weight * weight
            hit = row_ref[i, pl.ds(j, 1), :] == lax.broadcasted_iota(jnp.int32, (cells, slots), 0)
            density = jnp.sum(jnp.where(hit, square, 0.0), axis=1, keepdims=True)
            pulled = jnp.sum(
                jnp.where(hit, square * value_ref[i, pl.ds(j, 1), :], 0.0), axis=1, keepdims=True
            )
            out_ref[i, j, pl.ds(0, cells), :] = (jnp.sqrt(density) * pert).astype(BF16)
            side = jnp.sum(pert * (pulled - density * mean), axis=0, keepdims=True)
            high = side.astype(BF16).astype(F32)
            which = lax.broadcasted_iota(jnp.int32, (SIDE_ROWS, members), 0)
            tail = jnp.where(which == 0, high, jnp.where(which == 1, side - high, 0.0))
            out_ref[i, j, pl.ds(cells, SIDE_ROWS), :] = tail.astype(BF16)
        return carry

    lax.fori_loop(0, nodes // group, step, 0)


def edge_slices(step, size):
    if step == 0:
        return slice(0, size), slice(1, size + 1), size
    if step < 0:
        return 0, size + 1, 1
    return size - 1, 0, 1


def main_kernel(
    counts, qx_ref, state_ref, quadrant_ref, frac_lat_ref, frac_lon_ref, land_ref,
    out_ref, qbuf, wbuf, q_send, q_recv, w_send, w_recv, r_send, r_recv,
    c_send, c_recv,
):
    n_lat, n_lon = counts
    row_parts = r_send.shape[1]
    tile_lat, tile_lon, cells, members = state_ref.shape
    lat, lon = lax.axis_index("lat"), lax.axis_index("lon")

    def exists(way):
        if way[0] < 0:
            return lat > 0
        if way[0] > 0:
            return lat < n_lat - 1
        return None

    def where_exists(way, do):
        if way[0] == 0:
            do()
        else:
            pl.when(exists(way))(do)

    def peer(way):
        return (lat + way[0], lax.rem(lon + way[1] + n_lon, n_lon))

    def at(ref, i, j):
        i = pl.ds(i.start, i.stop - i.start) if isinstance(i, slice) else i
        j = pl.ds(j.start, j.stop - j.start) if isinstance(j, slice) else j
        return ref.at[i, j]

    def copy(source, offset, buffer, send, recv, index):
        way = WAYS[index]
        si, di, _ = edge_slices(way[0], tile_lat)
        sj, dj, _ = edge_slices(way[1], tile_lon)

        def moved(s):
            return slice(s.start + offset, s.stop + offset) if isinstance(s, slice) else s + offset

        return pltpu.make_async_remote_copy(
            src_ref=at(source, moved(si), moved(sj)),
            dst_ref=at(buffer, di, dj),
            send_sem=send.at[index],
            recv_sem=recv.at[index],
            device_id=peer(way),
            device_id_type=MESH,
        )

    def q_copy(index):
        return copy(qx_ref, 0, qbuf, q_send, q_recv, index)

    def w_copy(index):
        return copy(wbuf, 1, wbuf, w_send, w_recv, index)

    def row_copy(index, part):
        source, target, _ = edge_slices(WAYS[index][0], tile_lat)
        width = tile_lon // row_parts
        columns = pl.ds(1 + part * width, width)
        return pltpu.make_async_remote_copy(
            src_ref=wbuf.at[source + 1, columns],
            dst_ref=wbuf.at[target, columns],
            send_sem=r_send.at[index, part],
            recv_sem=r_recv.at[index, part],
            device_id=peer(WAYS[index]),
            device_id_type=MESH,
        )

    def corner_copy(buffer, stage, index):
        side, step = CORNERS[index]
        row = 0 if side < 0 else tile_lat + 1
        source, target = (1, tile_lon + 1) if step < 0 else (tile_lon, 0)
        return pltpu.make_async_remote_copy(
            src_ref=buffer.at[row, source],
            dst_ref=buffer.at[row, target],
            send_sem=c_send.at[stage, index],
            recv_sem=c_recv.at[stage, index],
            device_id=peer((0, step)),
            device_id_type=MESH,
        )

    def each_corner(buffer, stage, do):
        for index, way in enumerate(CORNERS):
            where_exists(way, lambda index=index: do(corner_copy(buffer, stage, index)))

    barrier = pltpu.get_barrier_semaphore()
    for way in WAYS:
        where_exists(way, lambda way=way: pl.semaphore_signal(
            barrier, inc=1, device_id=peer(way), device_id_type=MESH))
    present = 2 + (lat > 0).astype(jnp.int32) + (lat < n_lat - 1).astype(jnp.int32)
    pl.semaphore_wait(barrier, present)
    for index, way in enumerate(WAYS):
        where_exists(way, lambda index=index: q_copy(index).start())

    @pl.when(lat == 0)
    def _():
        qbuf[0] = jnp.zeros(qbuf.shape[1:], BF16)
        wbuf[0] = jnp.zeros(wbuf.shape[1:], BF16)

    @pl.when(lat == n_lat - 1)
    def _():
        qbuf[tile_lat + 1] = jnp.zeros(qbuf.shape[1:], BF16)
        wbuf[tile_lat + 1] = jnp.zeros(wbuf.shape[1:], BF16)

    for i in range(tile_lat):
        qbuf[i + 1, pl.ds(1, tile_lon)] = qx_ref[i]

    def received(index, make):
        way = WAYS[index]
        back = (-way[0], -way[1])
        where_exists(back, lambda: make(index).wait_recv())

    def sent(index, make):
        where_exists(WAYS[index], lambda: make(index).wait_send())

    eye = (
        lax.broadcasted_iota(jnp.int32, (members, members), 0)
        == lax.broadcasted_iota(jnp.int32, (members, members), 1)
    ).astype(F32)
    eye_b = eye.astype(BF16)

    def gram_of(i, j):
        left, right = [], []
        tail = jnp.zeros((SIDE_ROWS, members), F32)
        for b in range(3):
            for a in range(3):
                scale = NEAR[a] * NEAR[b]
                block = qbuf[i + a, j + b, pl.ds(0, cells), :]
                right.append(block)
                left.append(block if scale == 1.0 else block * jnp.asarray(scale, BF16))
                tail += scale * qbuf[i + a, j + b, pl.ds(cells, SIDE_ROWS), :].astype(F32)
        gram = tn(jnp.concatenate(left, axis=0), jnp.concatenate(right, axis=0))
        return gram, jnp.sum(tail, axis=0, keepdims=True)

    def total(x):
        return jnp.sum(jnp.sum(x, axis=0, keepdims=True), axis=1, keepdims=True)

    def transform(places):
        group = range(len(places))
        terms = [gram_of(i, j) for i, j in places]
        frobs, cy, ey, cz, ez = [], [], [], [], []
        for gram, _ in terms:
            ridge = members - 1.0
            trace = total(gram * eye)
            frob = jnp.sqrt(total(gram * gram) + 2.0 * ridge * trace + ridge * ridge * members)
            centre = ridge + trace * (1.0 / members)
            inv = 1.0 / centre
            rest = gram * inv + eye * (ridge * inv - 1.0)
            frobs.append(frob)
            start = centre / frob
            cf = 1.5 - 0.5 * start
            ef = rest * (-0.5 * start / cf)
            cy.append(cf * start)
            ey.append((ef + rest) + nn(ef.astype(BF16), rest.astype(BF16)))
            cz.append(cf)
            ez.append(ef)
        for step in range(1, ITERS):
            last = step == ITERS - 1
            ybs = [e.astype(BF16) for e in ey]
            zbs = [e.astype(BF16) for e in ez]
            prods = [nn(zb, yb) for zb, yb in zip(zbs, ybs)]
            cts = [y * z for y, z in zip(cy, cz)]
            cfs = [1.5 - 0.5 * ct for ct in cts]
            efs = [
                ((ey[n] + ez[n]) + prods[n]) * (-0.5 * cts[n] / cfs[n]) for n in group
            ]
            fbs = [e.astype(BF16) for e in efs]
            if last:
                both = [nn(fb, zb) for fb, zb in zip(fbs, zbs)]
            else:
                both = [
                    nn(fb, jnp.concatenate([zb, yb], axis=1))
                    for fb, zb, yb in zip(fbs, zbs, ybs)
                ]
            for n in group:
                if not last:
                    ey[n] = (efs[n] + ey[n]) + both[n][:, members:]
                    cy[n] = cfs[n] * cy[n]
                ez[n] = (efs[n] + ez[n]) + both[n][:, :members]
                cz[n] = cfs[n] * cz[n]
        which = lax.broadcasted_iota(jnp.int32, (SIDE_ROWS, members), 0)
        for n, (i, j) in enumerate(places):
            side = terms[n][1]
            zb = ez[n].astype(BF16)
            high = side.astype(BF16).astype(F32)
            rows = jnp.where(which == 0, high, jnp.where(which == 1, side - high, 0.0))
            inner = side + jnp.sum(nn(rows.astype(BF16), zb), axis=0, keepdims=True)
            inner = inner * (cz[n] * cz[n] / frobs[n])
            high = inner.astype(BF16)
            low = (inner - high.astype(F32)).astype(BF16)
            high = jnp.broadcast_to(high, (members, members))
            low = jnp.broadcast_to(low, (members, members))
            mean_weight = nt(
                jnp.concatenate([zb, eye_b, eye_b], axis=1),
                jnp.concatenate([high, high, low], axis=1),
            )
            spread = math.sqrt(members - 1) * cz[n] / jnp.sqrt(frobs[n])
            wbuf[i + 1, j + 1] = (mean_weight + spread * (ez[n] + eye)).astype(BF16)

    mid_lat, mid_lon = tile_lat - 2, tile_lon - 2
    n_rows, n_sides, n_inner = 2 * tile_lon, 2 * mid_lat, mid_lat * mid_lon
    group = n_rows // row_parts
    ahead = 2 * (n_inner // group) // 3
    g_rows, g_sides, g_inner = n_rows // group, n_sides // group, n_inner // group

    def row_place(k):
        return (k % 2) * (tile_lat - 1), k // 2

    def side_place(k):
        return 1 + k // 2, (k % 2) * (tile_lon - 1)

    def inner_place(k):
        return 1 + k // mid_lon, 1 + k % mid_lon

    def place(slot, g):
        rows = slot - ahead
        sides = rows - g_rows
        after = slot - g_rows - g_sides
        is_inner = (slot < ahead) | (sides >= g_sides)
        inner = inner_place(jnp.where(slot < ahead, slot, jnp.maximum(after, 0)) * group + g)
        row = row_place(jnp.clip(rows, 0, g_rows - 1) * group + g)
        side = side_place(jnp.clip(sides, 0, g_sides - 1) * group + g)
        i = jnp.where(is_inner, inner[0], jnp.where(sides >= 0, side[0], row[0]))
        j = jnp.where(is_inner, inner[1], jnp.where(sides >= 0, side[1], row[1]))
        return i, j

    def node_step(slot, carry):
        @pl.when(slot == ahead // 2)
        def _():
            for index in range(2):
                received(index, q_copy)
            each_corner(qbuf, 0, lambda copy: copy.start())

        @pl.when(slot == ahead)
        def _():
            for index in range(2, 4):
                received(index, q_copy)
            each_corner(qbuf, 0, lambda copy: copy.wait_recv())

        transform([place(slot, g) for g in range(group)])

        for index in range(2):
            part = slot - ahead
            pl.when(exists(WAYS[index]) & (part >= 0) & (part < g_rows))(
                lambda index=index, part=part: row_copy(index, part).start())

        @pl.when(slot == ahead + g_rows + g_sides - 1)
        def _():
            for index in range(2, 4):
                w_copy(index).start()

        return carry

    lax.fori_loop(0, g_rows + g_sides + g_inner, node_step, 0)

    def analyse(i, j):
        values = state_ref[i, j].astype(F32)
        mean = jnp.sum(values, axis=1, keepdims=True) * (1.0 / members)
        pert = (values - mean).astype(BF16)
        corner = quadrant_ref[i, pl.ds(j, 1), :]
        along = []
        for half, frac in (
            (corner // 2, frac_lat_ref[i, pl.ds(j, 1), :]),
            (corner % 2, frac_lon_ref[i, pl.ds(j, 1), :]),
        ):
            for a in range(3):
                along.append(
                    jnp.where(half == a, 1.0 - frac, 0.0) + jnp.where(half + 1 == a, frac, 0.0)
                )
        along.append(land_ref[i, pl.ds(j, 1), :].astype(F32))
        along.append(jnp.zeros_like(along[0]))
        coef = jnp.transpose(jnp.concatenate(along, axis=0))
        acc = mean
        for a in range(3):
            wide = jnp.concatenate([wbuf[i + a, j + b] for b in range(3)], axis=1)
            prod = nn(pert, wide)
            row = sum(
                coef[:, 3 + b : 4 + b] * prod[:, b * members : (b + 1) * members] for b in range(3)
            )
            acc = acc + coef[:, a : a + 1] * row
        result = jnp.where(coef[:, 6:7] == 1.0, acc, values)
        out_ref[i, j] = result.astype(BF16)

    def inner_step(t, carry):
        for g in range(group):
            analyse(*inner_place(t * group + g))
        return carry

    lax.fori_loop(0, g_inner, inner_step, 0)
    for index in range(2):
        for part in range(row_parts):
            received(index, lambda index, part=part: row_copy(index, part))
    each_corner(wbuf, 1, lambda copy: copy.start())
    for index in range(2, len(WAYS)):
        received(index, w_copy)

    def rim_step(t, carry):
        @pl.when(t == g_sides + row_parts - 2)
        def _():
            each_corner(wbuf, 1, lambda copy: copy.wait_recv())

        part = lax.rem(t - g_sides + 1 + row_parts, row_parts)
        first = jnp.where(t < g_sides, n_rows + t * group, part * group)
        for g in range(group):
            k = first + g
            row, side = row_place(jnp.minimum(k, n_rows - 1)), side_place(jnp.maximum(k - n_rows, 0))
            analyse(jnp.where(k < n_rows, row[0], side[0]), jnp.where(k < n_rows, row[1], side[1]))
        return carry

    lax.fori_loop(0, g_rows + g_sides, rim_step, 0)
    for index in range(len(WAYS)):
        sent(index, q_copy)
        if index >= 2:
            sent(index, w_copy)
        else:
            for part in range(row_parts):
                sent(index, lambda index, part=part: row_copy(index, part))
    each_corner(qbuf, 0, lambda copy: copy.wait_send())
    each_corner(wbuf, 1, lambda copy: copy.wait_send())


VM = pl.BlockSpec(memory_space=pltpu.VMEM)


def body(counts, state, obs_row, obs_count, obs_value, obs_weight, quadrant, frac_lat, frac_lon, land):
    tile_lat, tile_lon, cells, members = state.shape
    rows = cells + SIDE_ROWS
    sizes = (2 * tile_lon, 2 * (tile_lat - 2), (tile_lat - 2) * (tile_lon - 2))
    row_parts = 2 * tile_lon // next(g for g in (4, 2) if all(n % g == 0 for n in sizes))
    qx = pl.pallas_call(
        prep_kernel,
        out_shape=jax.ShapeDtypeStruct((tile_lat, tile_lon, rows, members), BF16),
        in_specs=[pl.BlockSpec(memory_space=pltpu.SMEM)] + [VM] * 4,
        out_specs=VM,
        name="prep",
    )(obs_count, state, obs_row, obs_value, obs_weight)
    return pl.pallas_call(
        functools.partial(main_kernel, counts),
        out_shape=jax.ShapeDtypeStruct(state.shape, BF16),
        in_specs=[VM] * 6,
        out_specs=VM,
        scratch_shapes=[
            pltpu.VMEM((tile_lat + 2, tile_lon + 2, rows, members), BF16),
            pltpu.VMEM((tile_lat + 2, tile_lon + 2, members, members), BF16),
            pltpu.SemaphoreType.DMA((4,)),
            pltpu.SemaphoreType.DMA((4,)),
            pltpu.SemaphoreType.DMA((4,)),
            pltpu.SemaphoreType.DMA((4,)),
            pltpu.SemaphoreType.DMA((2, row_parts)),
            pltpu.SemaphoreType.DMA((2, row_parts)),
            pltpu.SemaphoreType.DMA((2, 4)),
            pltpu.SemaphoreType.DMA((2, 4)),
        ],
        compiler_params=pltpu.CompilerParams(
            collective_id=0, has_side_effects=True, vmem_limit_bytes=48 * 1024 * 1024
        ),
        name="analyse",
    )(qx, state, quadrant, frac_lat, frac_lon, land)


def solution(mesh):
    counts = (mesh.shape["lat"], mesh.shape["lon"])
    return jax.shard_map(
        functools.partial(body, counts),
        mesh=mesh,
        in_specs=(
            P("lat", "lon", None, None),
            P("lat", "lon", None),
            P("lat", "lon"),
            P("lat", "lon", None),
            P("lat", "lon", None),
            P("lat", "lon", None),
            P("lat", "lon", None),
            P("lat", "lon", None),
            P("lat", "lon", None),
        ),
        out_specs=P("lat", "lon", None, None),
        check_vma=False,
    )
```

```python
import functools
import math

import jax
import jax.numpy as jnp
from jax import lax
from jax.experimental import pallas as pl
from jax.experimental.pallas import tpu as pltpu
from jax.sharding import PartitionSpec as P

ITERS = 6
NEAR = (0.5, 1.0, 0.5)
SIDE_ROWS = 8
F32 = jnp.float32
BF16 = jnp.bfloat16
MESH = pl.DeviceIdType.MESH
WAYS = ((-1, 0), (1, 0), (0, -1), (0, 1))
CORNERS = ((-1, -1), (-1, 1), (1, -1), (1, 1))


def nn(a, b):
    return lax.dot_general(a, b, (((1,), (0,)), ((), ())), preferred_element_type=F32)


def nt(a, b):
    return lax.dot_general(a, b, (((1,), (1,)), ((), ())), preferred_element_type=F32)


def tn(a, b):
    return lax.dot_general(a, b, (((0,), (0,)), ((), ())), preferred_element_type=F32)


def group_of(count, most=4):
    return next(g for g in range(most, 0, -1) if count % g == 0)


def prep_kernel(count_ref, state_ref, row_ref, value_ref, weight_ref, out_ref):
    tile_lat, tile_lon, cells, members = state_ref.shape
    slots = row_ref.shape[-1]
    nodes = tile_lat * tile_lon
    group = group_of(nodes, 8)

    def step(t, carry):
        for g in range(group):
            node = t * group + g
            i, j = node // tile_lon, node % tile_lon
            values = state_ref[i, j].astype(F32)
            mean = jnp.sum(values, axis=1, keepdims=True) * (1.0 / members)
            pert = values - mean
            lane = lax.broadcasted_iota(jnp.int32, (1, slots), 1)
            weight = jnp.where(lane < count_ref[i, j], weight_ref[i, pl.ds(j, 1), :], 0.0)
            square = weight * weight
            hit = row_ref[i, pl.ds(j, 1), :] == lax.broadcasted_iota(jnp.int32, (cells, slots), 0)
            density = jnp.sum(jnp.where(hit, square, 0.0), axis=1, keepdims=True)
            pulled = jnp.sum(
                jnp.where(hit, square * value_ref[i, pl.ds(j, 1), :], 0.0), axis=1, keepdims=True
            )
            out_ref[i, j, pl.ds(0, cells), :] = (jnp.sqrt(density) * pert).astype(BF16)
            side = jnp.sum(pert * (pulled - density * mean), axis=0, keepdims=True)
            high = side.astype(BF16).astype(F32)
            which = lax.broadcasted_iota(jnp.int32, (SIDE_ROWS, members), 0)
            tail = jnp.where(which == 0, high, jnp.where(which == 1, side - high, 0.0))
            out_ref[i, j, pl.ds(cells, SIDE_ROWS), :] = tail.astype(BF16)
        return carry

    lax.fori_loop(0, nodes // group, step, 0)


def edge_slices(step, size):
    if step == 0:
        return slice(0, size), slice(1, size + 1), size
    if step < 0:
        return 0, size + 1, 1
    return size - 1, 0, 1


def main_kernel(
    counts, qx_ref, state_ref, quadrant_ref, frac_lat_ref, frac_lon_ref, land_ref,
    out_ref, qbuf, wbuf, q_send, q_recv, w_send, w_recv, r_send, r_recv,
    c_send, c_recv,
):
    n_lat, n_lon = counts
    row_parts = r_send.shape[1]
    tile_lat, tile_lon, cells, members = state_ref.shape
    lat, lon = lax.axis_index("lat"), lax.axis_index("lon")

    def exists(way):
        if way[0] < 0:
            return lat > 0
        if way[0] > 0:
            return lat < n_lat - 1
        return None

    def where_exists(way, do):
        if way[0] == 0:
            do()
        else:
            pl.when(exists(way))(do)

    def peer(way):
        return (lat + way[0], lax.rem(lon + way[1] + n_lon, n_lon))

    def at(ref, i, j):
        i = pl.ds(i.start, i.stop - i.start) if isinstance(i, slice) else i
        j = pl.ds(j.start, j.stop - j.start) if isinstance(j, slice) else j
        return ref.at[i, j]

    def copy(source, offset, buffer, send, recv, index):
        way = WAYS[index]
        si, di, _ = edge_slices(way[0], tile_lat)
        sj, dj, _ = edge_slices(way[1], tile_lon)

        def moved(s):
            return slice(s.start + offset, s.stop + offset) if isinstance(s, slice) else s + offset

        return pltpu.make_async_remote_copy(
            src_ref=at(source, moved(si), moved(sj)),
            dst_ref=at(buffer, di, dj),
            send_sem=send.at[index],
            recv_sem=recv.at[index],
            device_id=peer(way),
            device_id_type=MESH,
        )

    def q_copy(index):
        return copy(qx_ref, 0, qbuf, q_send, q_recv, index)

    def w_copy(index):
        return copy(wbuf, 1, wbuf, w_send, w_recv, index)

    def row_copy(index, part):
        source, target, _ = edge_slices(WAYS[index][0], tile_lat)
        width = tile_lon // row_parts
        columns = pl.ds(1 + part * width, width)
        return pltpu.make_async_remote_copy(
            src_ref=wbuf.at[source + 1, columns],
            dst_ref=wbuf.at[target, columns],
            send_sem=r_send.at[index, part],
            recv_sem=r_recv.at[index, part],
            device_id=peer(WAYS[index]),
            device_id_type=MESH,
        )

    def corner_copy(buffer, stage, index):
        side, step = CORNERS[index]
        row = 0 if side < 0 else tile_lat + 1
        source, target = (1, tile_lon + 1) if step < 0 else (tile_lon, 0)
        return pltpu.make_async_remote_copy(
            src_ref=buffer.at[row, source],
            dst_ref=buffer.at[row, target],
            send_sem=c_send.at[stage, index],
            recv_sem=c_recv.at[stage, index],
            device_id=peer((0, step)),
            device_id_type=MESH,
        )

    def each_corner(buffer, stage, do):
        for index, way in enumerate(CORNERS):
            where_exists(way, lambda index=index: do(corner_copy(buffer, stage, index)))

    barrier = pltpu.get_barrier_semaphore()
    for way in WAYS:
        where_exists(way, lambda way=way: pl.semaphore_signal(
            barrier, inc=1, device_id=peer(way), device_id_type=MESH))
    present = 2 + (lat > 0).astype(jnp.int32) + (lat < n_lat - 1).astype(jnp.int32)
    pl.semaphore_wait(barrier, present)
    for index, way in enumerate(WAYS):
        where_exists(way, lambda index=index: q_copy(index).start())

    @pl.when(lat == 0)
    def _():
        qbuf[0] = jnp.zeros(qbuf.shape[1:], BF16)
        wbuf[0] = jnp.zeros(wbuf.shape[1:], BF16)

    @pl.when(lat == n_lat - 1)
    def _():
        qbuf[tile_lat + 1] = jnp.zeros(qbuf.shape[1:], BF16)
        wbuf[tile_lat + 1] = jnp.zeros(wbuf.shape[1:], BF16)

    for i in range(tile_lat):
        qbuf[i + 1, pl.ds(1, tile_lon)] = qx_ref[i]

    def received(index, make):
        way = WAYS[index]
        back = (-way[0], -way[1])
        where_exists(back, lambda: make(index).wait_recv())

    def sent(index, make):
        where_exists(WAYS[index], lambda: make(index).wait_send())

    eye = (
        lax.broadcasted_iota(jnp.int32, (members, members), 0)
        == lax.broadcasted_iota(jnp.int32, (members, members), 1)
    ).astype(F32)
    eye_b = eye.astype(BF16)

    def gram_of(i, j):
        left, right = [], []
        tail = jnp.zeros((SIDE_ROWS, members), F32)
        for b in range(3):
            for a in range(3):
                scale = NEAR[a] * NEAR[b]
                block = qbuf[i + a, j + b, pl.ds(0, cells), :]
                right.append(block)
                left.append(block if scale == 1.0 else block * jnp.asarray(scale, BF16))
                tail += scale * qbuf[i + a, j + b, pl.ds(cells, SIDE_ROWS), :].astype(F32)
        gram = tn(jnp.concatenate(left, axis=0), jnp.concatenate(right, axis=0))
        return gram, jnp.sum(tail, axis=0, keepdims=True)

    def total(x):
        return jnp.sum(jnp.sum(x, axis=0, keepdims=True), axis=1, keepdims=True)

    def transform(places):
        group = range(len(places))
        terms = [gram_of(i, j) for i, j in places]
        frobs, cy, ey, cz, ez = [], [], [], [], []
        for gram, _ in terms:
            ridge = members - 1.0
            trace = total(gram * eye)
            frob = jnp.sqrt(total(gram * gram) + 2.0 * ridge * trace + ridge * ridge * members)
            centre = ridge + trace * (1.0 / members)
            inv = 1.0 / centre
            rest = gram * inv + eye * (ridge * inv - 1.0)
            frobs.append(frob)
            start = centre / frob
            cf = 1.5 - 0.5 * start
            ef = rest * (-0.5 * start / cf)
            cy.append(cf * start)
            ey.append((ef + rest) + nn(ef.astype(BF16), rest.astype(BF16)))
            cz.append(cf)
            ez.append(ef)
        for step in range(1, ITERS):
            last = step == ITERS - 1
            ybs = [e.astype(BF16) for e in ey]
            zbs = [e.astype(BF16) for e in ez]
            prods = [nn(zb, yb) for zb, yb in zip(zbs, ybs)]
            cts = [y * z for y, z in zip(cy, cz)]
            cfs = [1.5 - 0.5 * ct for ct in cts]
            efs = [
                ((ey[n] + ez[n]) + prods[n]) * (-0.5 * cts[n] / cfs[n]) for n in group
            ]
            fbs = [e.astype(BF16) for e in efs]
            if last:
                both = [nn(fb, zb) for fb, zb in zip(fbs, zbs)]
            else:
                both = [
                    nn(fb, jnp.concatenate([zb, yb], axis=1))
                    for fb, zb, yb in zip(fbs, zbs, ybs)
                ]
            for n in group:
                if not last:
                    ey[n] = (efs[n] + ey[n]) + both[n][:, members:]
                    cy[n] = cfs[n] * cy[n]
                ez[n] = (efs[n] + ez[n]) + both[n][:, :members]
                cz[n] = cfs[n] * cz[n]
        which = lax.broadcasted_iota(jnp.int32, (SIDE_ROWS, members), 0)
        for n, (i, j) in enumerate(places):
            side = terms[n][1]
            zb = ez[n].astype(BF16)
            high = side.astype(BF16).astype(F32)
            rows = jnp.where(which == 0, high, jnp.where(which == 1, side - high, 0.0))
            inner = side + jnp.sum(nn(rows.astype(BF16), zb), axis=0, keepdims=True)
            inner = inner * (cz[n] * cz[n] / frobs[n])
            high = inner.astype(BF16)
            low = (inner - high.astype(F32)).astype(BF16)
            high = jnp.broadcast_to(high, (members, members))
            low = jnp.broadcast_to(low, (members, members))
            mean_weight = nt(
                jnp.concatenate([zb, eye_b, eye_b], axis=1),
                jnp.concatenate([high, high, low], axis=1),
            )
            spread = math.sqrt(members - 1) * cz[n] / jnp.sqrt(frobs[n])
            wbuf[i + 1, j + 1] = (mean_weight + spread * (ez[n] + eye)).astype(BF16)

    mid_lat, mid_lon = tile_lat - 2, tile_lon - 2
    n_rows, n_sides, n_inner = 2 * tile_lon, 2 * mid_lat, mid_lat * mid_lon
    group = n_rows // row_parts
    ahead = n_inner // group
    g_rows, g_sides, g_inner = n_rows // group, n_sides // group, n_inner // group

    def row_place(k):
        return (k % 2) * (tile_lat - 1), k // 2

    def side_place(k):
        return 1 + k // 2, (k % 2) * (tile_lon - 1)

    def inner_place(k):
        return 1 + k // mid_lon, 1 + k % mid_lon

    def place(slot, g):
        rows = slot - ahead
        sides = rows - g_rows
        after = slot - g_rows - g_sides
        is_inner = (slot < ahead) | (sides >= g_sides)
        inner = inner_place(jnp.where(slot < ahead, slot, jnp.maximum(after, 0)) * group + g)
        row = row_place(jnp.clip(rows, 0, g_rows - 1) * group + g)
        side = side_place(jnp.clip(sides, 0, g_sides - 1) * group + g)
        i = jnp.where(is_inner, inner[0], jnp.where(sides >= 0, side[0], row[0]))
        j = jnp.where(is_inner, inner[1], jnp.where(sides >= 0, side[1], row[1]))
        return i, j

    def node_step(slot, carry):
        @pl.when(slot == ahead - 1)
        def _():
            for index in range(2):
                received(index, q_copy)
            each_corner(qbuf, 0, lambda copy: copy.start())

        @pl.when(slot == ahead)
        def _():
            for index in range(2, 4):
                received(index, q_copy)
            each_corner(qbuf, 0, lambda copy: copy.wait_recv())

        transform([place(slot, g) for g in range(group)])

        for index in range(2):
            part = slot - ahead
            pl.when(exists(WAYS[index]) & (part >= 0) & (part < g_rows))(
                lambda index=index, part=part: row_copy(index, part).start())

        @pl.when(slot == ahead + g_rows + g_sides - 1)
        def _():
            for index in range(2, 4):
                w_copy(index).start()

        return carry

    lax.fori_loop(0, g_rows + g_sides + g_inner, node_step, 0)

    def analyse(i, j):
        values = state_ref[i, j].astype(F32)
        mean = jnp.sum(values, axis=1, keepdims=True) * (1.0 / members)
        pert = (values - mean).astype(BF16)
        corner = quadrant_ref[i, pl.ds(j, 1), :]
        along = []
        for half, frac in (
            (corner // 2, frac_lat_ref[i, pl.ds(j, 1), :]),
            (corner % 2, frac_lon_ref[i, pl.ds(j, 1), :]),
        ):
            for a in range(3):
                along.append(
                    jnp.where(half == a, 1.0 - frac, 0.0) + jnp.where(half + 1 == a, frac, 0.0)
                )
        along.append(land_ref[i, pl.ds(j, 1), :].astype(F32))
        along.append(jnp.zeros_like(along[0]))
        coef = jnp.transpose(jnp.concatenate(along, axis=0))
        acc = mean
        for a in range(3):
            wide = jnp.concatenate([wbuf[i + a, j + b] for b in range(3)], axis=1)
            prod = nn(pert, wide)
            row = sum(
                coef[:, 3 + b : 4 + b] * prod[:, b * members : (b + 1) * members] for b in range(3)
            )
            acc = acc + coef[:, a : a + 1] * row
        result = jnp.where(coef[:, 6:7] == 1.0, acc, values)
        out_ref[i, j] = result.astype(BF16)

    def inner_step(t, carry):
        for g in range(group):
            analyse(*inner_place(t * group + g))
        return carry

    lax.fori_loop(0, g_inner, inner_step, 0)
    for index in range(2):
        for part in range(row_parts):
            received(index, lambda index, part=part: row_copy(index, part))
    each_corner(wbuf, 1, lambda copy: copy.start())
    for index in range(2, len(WAYS)):
        received(index, w_copy)

    def rim_step(t, carry):
        @pl.when(t == g_sides + row_parts - 2)
        def _():
            each_corner(wbuf, 1, lambda copy: copy.wait_recv())

        part = lax.rem(t - g_sides + 1 + row_parts, row_parts)
        first = jnp.where(t < g_sides, n_rows + t * group, part * group)
        for g in range(group):
            k = first + g
            row, side = row_place(jnp.minimum(k, n_rows - 1)), side_place(jnp.maximum(k - n_rows, 0))
            analyse(jnp.where(k < n_rows, row[0], side[0]), jnp.where(k < n_rows, row[1], side[1]))
        return carry

    lax.fori_loop(0, g_rows + g_sides, rim_step, 0)
    for index in range(len(WAYS)):
        sent(index, q_copy)
        if index >= 2:
            sent(index, w_copy)
        else:
            for part in range(row_parts):
                sent(index, lambda index, part=part: row_copy(index, part))
    each_corner(qbuf, 0, lambda copy: copy.wait_send())
    each_corner(wbuf, 1, lambda copy: copy.wait_send())


VM = pl.BlockSpec(memory_space=pltpu.VMEM)


def body(counts, state, obs_row, obs_count, obs_value, obs_weight, quadrant, frac_lat, frac_lon, land):
    tile_lat, tile_lon, cells, members = state.shape
    rows = cells + SIDE_ROWS
    sizes = (2 * tile_lon, 2 * (tile_lat - 2), (tile_lat - 2) * (tile_lon - 2))
    row_parts = 2 * tile_lon // next(g for g in (4, 2) if all(n % g == 0 for n in sizes))
    qx = pl.pallas_call(
        prep_kernel,
        out_shape=jax.ShapeDtypeStruct((tile_lat, tile_lon, rows, members), BF16),
        in_specs=[pl.BlockSpec(memory_space=pltpu.SMEM)] + [VM] * 4,
        out_specs=VM,
        name="prep",
    )(obs_count, state, obs_row, obs_value, obs_weight)
    return pl.pallas_call(
        functools.partial(main_kernel, counts),
        out_shape=jax.ShapeDtypeStruct(state.shape, BF16),
        in_specs=[VM] * 6,
        out_specs=VM,
        scratch_shapes=[
            pltpu.VMEM((tile_lat + 2, tile_lon + 2, rows, members), BF16),
            pltpu.VMEM((tile_lat + 2, tile_lon + 2, members, members), BF16),
            pltpu.SemaphoreType.DMA((4,)),
            pltpu.SemaphoreType.DMA((4,)),
            pltpu.SemaphoreType.DMA((4,)),
            pltpu.SemaphoreType.DMA((4,)),
            pltpu.SemaphoreType.DMA((2, row_parts)),
            pltpu.SemaphoreType.DMA((2, row_parts)),
            pltpu.SemaphoreType.DMA((2, 4)),
            pltpu.SemaphoreType.DMA((2, 4)),
        ],
        compiler_params=pltpu.CompilerParams(
            collective_id=0, has_side_effects=True, vmem_limit_bytes=48 * 1024 * 1024
        ),
        name="analyse",
    )(qx, state, quadrant, frac_lat, frac_lon, land)


def solution(mesh):
    counts = (mesh.shape["lat"], mesh.shape["lon"])
    return jax.shard_map(
        functools.partial(body, counts),
        mesh=mesh,
        in_specs=(
            P("lat", "lon", None, None),
            P("lat", "lon", None),
            P("lat", "lon"),
            P("lat", "lon", None),
            P("lat", "lon", None),
            P("lat", "lon", None),
            P("lat", "lon", None),
            P("lat", "lon", None),
            P("lat", "lon", None),
        ),
        out_specs=P("lat", "lon", None, None),
        check_vma=False,
    )
```
